128 devices in a mesh: dp: 16 (over y_hi, x, core), tensor: 8 (over z, y_lo).
Axes of the slice: x: 4, y: 4 (y_hi: 2, y_lo: 2; y = y_hi * 2 + y_lo), z: 4, core: 2. Of those that a mesh axis runs over, the one named last changes fastest.
Arguments:
- cand_gate: bfloat16 [4096, 28672], P('dp', 'tensor'), may hold values from -6 to 6
- cand_up: bfloat16 [4096, 28672], P('dp', 'tensor'), may hold values from -6 to 6
- cand_dh: bfloat16 [4096, 28672], P('dp', 'tensor'), may hold values from -6 to 6
- cand_x: bfloat16 [4096, 8192], P('dp', 'tensor'), may hold values from -6 to 6
- cand_dy: bfloat16 [4096, 8192], P('dp', 'tensor'), may hold values from -6 to 6
- val_gate: bfloat16 [4096, 28672], P('dp', 'tensor'), may hold values from -6 to 6
- val_up: bfloat16 [4096, 28672], P('dp', 'tensor'), may hold values from -6 to 6
- val_dh: bfloat16 [4096, 28672], P('dp', 'tensor'), may hold values from -6 to 6
- val_x: bfloat16 [4096, 8192], P('dp', 'tensor'), may hold values from -6 to 6
- val_dy: bfloat16 [4096, 8192], P('dp', 'tensor'), may hold values from -6 to 6
- cand_lengths: int32 [16, 8], P('dp'), may hold values from 1 to 64, 256 in all within a row
- val_lengths: int32 [16, 8], replicated, may hold values from 1 to 64, 256 in all within a row
- round_owner: int32 [2], replicated, may hold values from 0 to 15
Outputs:
- scores: float32 [2, 128, 8], P(None, 'dp')
The draws below stay inside these ranges and needn't reach their ends.
Inputs may be any that keep to these rules, and one draw needn't show every extreme that they name: Each row of cand_lengths sums to 256, and its largest entry is 64. Each row of val_lengths sums to 256, and its largest entry is 64.
All inputs are finite; a program needn't handle non-finite values.
Results may differ from the reference program's by a relative error of at most 0.0042.
Values may be sent and summed in bfloat16 or wider, within the bound.
A program may use at most 128 MiB of HBM per device.

```python
import math
import jax
import jax.numpy as jnp
import numpy as np
from jax import lax

D = 8192
FF = 28672
CAND_DEV = 256
VAL_DEV = 256
CSAMP = 8
VSAMP = 8
ROUNDS = 2
CAND_TOK = 4096
VAL_TOK = 4096
N_DP = 16


def shard_levels(own_key, extent, split, low, top_value):
    def one(axis_at, parts):
        draws = jax.random.uniform(jax.random.fold_in(jax.random.fold_in(own_key, 6), axis_at), (parts,), jnp.float32, low / len(split), top_value / len(split))
        return jnp.repeat(jnp.exp(draws), extent[axis_at] // parts).reshape((-1,) + (1,) * (len(extent) - axis_at - 1))

    loudness = one(*split[0])
    for cut in split[1:]:
        loudness = loudness * one(*cut)
    return loudness


def length_profile(count, total, bound, slope):
    weights = [(1 << 20) // math.isqrt(standing ** slope) + 1 for standing in range(2, count + 1)]
    spare, given = total - bound - (count - 1), [1] * (count - 1)
    while spare > 0:
        candidates = [i for i in range(count - 1) if given[i] < bound]
        mass, remaining = sum([weights[i] for i in candidates]), spare
        for i in candidates:
            extra = min(bound - given[i], max(1, remaining * weights[i] // mass), spare)
            given[i] = given[i] + extra
            spare = spare - extra
    return np.array([bound] + given)


def uneven(key, number_of, total, most, skew):
    if number_of == 2:
        one = jax.random.randint(key, (), max(1, total - most), min(most, total - 1) + 1)
        return jnp.stack([one, total - one])
    sizes = jnp.asarray(length_profile(number_of, total, most, skew), jnp.int32)
    pairs = (number_of - 1) // 2
    source_of, sink = sizes[1:1 + 2 * pairs:2], sizes[2:2 + 2 * pairs:2]
    margin = jnp.minimum(source_of - 1, most - sink)
    passed = jax.random.randint(jax.random.fold_in(key, 1), (pairs,), 0, 1 << 20) % (margin + 1)
    sizes = sizes.at[1:1 + 2 * pairs:2].set(source_of - passed).at[2:2 + 2 * pairs:2].set(sink + passed)
    return sizes[jax.random.permutation(jax.random.fold_in(key, 2), number_of)]


def centred(stream_key, dims, scale, bound, pieces=(), held_as=jnp.bfloat16):
    values = jax.random.normal(stream_key, dims, jnp.float32) * scale
    if len(pieces) > 0:
        values = shard_levels(stream_key, dims, pieces, -0.22, 0.18) * values
    return jnp.clip(values, min=-bound, max=bound).astype(held_as)


def setup_inputs(seed: int = 0) -> dict:
    key_list = jax.random.split(jax.random.key(seed), 14)
    cand_gate = centred(key_list[0], (CAND_TOK, FF), 1.0, 6.0, ((0, 16), (1, 8)))
    cand_up = centred(key_list[1], (CAND_TOK, FF), 1.0, 6.0, ((0, 16), (1, 8)))
    cand_dh = centred(key_list[2], (CAND_TOK, FF), 1.0, 6.0, ((0, 16), (1, 8)))
    cand_x = centred(key_list[3], (CAND_TOK, D), 1.0, 6.0, ((0, 16), (1, 8)))
    cand_dy = centred(key_list[4], (CAND_TOK, D), 1.0, 6.0, ((0, 16), (1, 8)))
    val_gate = centred(key_list[5], (VAL_TOK, FF), 1.0, 6.0, ((0, 16), (1, 8)))
    val_up = centred(key_list[6], (VAL_TOK, FF), 1.0, 6.0, ((0, 16), (1, 8)))
    val_dh = centred(key_list[7], (VAL_TOK, FF), 1.0, 6.0, ((0, 16), (1, 8)))
    val_x = centred(key_list[8], (VAL_TOK, D), 1.0, 6.0, ((0, 16), (1, 8)))
    val_dy = centred(key_list[9], (VAL_TOK, D), 1.0, 6.0, ((0, 16), (1, 8)))
    cand_lengths = jax.vmap(lambda own: uneven(own, CSAMP, CAND_DEV, CAND_DEV // 4, 2))(jax.random.split(key_list[10], N_DP)).reshape((N_DP, CSAMP)).astype(jnp.int32)
    val_lengths = jax.vmap(lambda own: uneven(own, VSAMP, VAL_DEV, VAL_DEV // 4, 2))(jax.random.split(key_list[11], N_DP)).reshape((N_DP, VSAMP)).astype(jnp.int32)
    round_owner = jax.random.randint(key_list[12], (ROUNDS,), 0, N_DP).astype(jnp.int32)
    return dict(cand_gate=cand_gate, cand_up=cand_up, cand_dh=cand_dh, cand_x=cand_x, cand_dy=cand_dy, val_gate=val_gate, val_up=val_up, val_dh=val_dh, val_x=val_x, val_dy=val_dy, cand_lengths=cand_lengths, val_lengths=val_lengths, round_owner=round_owner)


def derive(gate, up, grad_hidden):
    gate_f = gate.astype(jnp.float32)
    up_f = up.astype(jnp.float32)
    grad_f = grad_hidden.astype(jnp.float32)
    sigmoid_gate = jax.nn.sigmoid(gate_f)
    activated = gate_f * sigmoid_gate
    hidden = (activated * up_f).astype(jnp.bfloat16)
    grad_gate = (grad_f * up_f * sigmoid_gate * (1.0 + gate_f * (1.0 - sigmoid_gate))).astype(jnp.bfloat16)
    grad_up = (grad_f * activated).astype(jnp.bfloat16)
    return (grad_gate, grad_up, hidden)

def onehot(lengths, total):
    bounds = jnp.cumsum(lengths.astype(jnp.int32))
    position = jnp.arange(total, dtype=jnp.int32)
    segment = lax.optimization_barrier(jnp.sum((position[:, None] >= bounds[None, :]).astype(jnp.int32), axis=1))
    labels = jnp.arange(lengths.shape[0], dtype=jnp.int32)
    return (segment[:, None] == labels[None, :]).astype(jnp.float32)

def gram(left, right):
    return jnp.dot(left, right.T, preferred_element_type=jnp.float32)

def reference(cand_gate, cand_up, cand_dh, cand_x, cand_dy, val_gate, val_up, val_dh, val_x, val_dy, cand_lengths, val_lengths, round_owner):
    score_scale = 1.0 / math.sqrt(D * FF)
    blocks = (cand_gate.reshape(N_DP, CAND_DEV, FF), cand_up.reshape(N_DP, CAND_DEV, FF), cand_dh.reshape(N_DP, CAND_DEV, FF), cand_x.reshape(N_DP, CAND_DEV, D), cand_dy.reshape(N_DP, CAND_DEV, D), cand_lengths)
    results = []
    for round_index in range(ROUNDS):
        owner_index = round_owner[round_index]
        first_row = (owner_index * VAL_DEV).astype(jnp.int32)

        def pick(array):
            return lax.dynamic_slice_in_dim(array, first_row, VAL_DEV, 0)
        val_gd, val_ud, val_hidden = derive(pick(val_gate), pick(val_up), pick(val_dh))
        val_gu = jnp.concatenate([val_gd, val_ud], axis=1)
        val_xs = pick(val_x)
        val_dys = pick(val_dy)
        val_len = lax.dynamic_index_in_dim(val_lengths, owner_index.astype(jnp.int32), 0, keepdims=False)
        val_hot = onehot(val_len, VAL_DEV)
        val_count = val_len.astype(jnp.float32)

        def member(items):
            gate, up, grad_hidden, inputs, grad_out, lengths = items
            grad_gate, grad_up, hidden = derive(gate, up, grad_hidden)
            cand_gu = jnp.concatenate([grad_gate, grad_up], axis=1)
            pair = gram(inputs, val_xs) * gram(cand_gu, val_gu) + gram(hidden, val_hidden) * gram(grad_out, val_dys)
            cand_hot = onehot(lengths, CAND_DEV)
            summed = jnp.dot(cand_hot.T, pair, precision=lax.Precision.HIGHEST)
            summed = jnp.dot(summed, val_hot, precision=lax.Precision.HIGHEST)
            cand_count = lengths.astype(jnp.float32)
            return summed * score_scale / jnp.sqrt(cand_count[:, None] * val_count[None, :])
        per_member = lax.map(member, blocks)
        results.append(per_member.reshape(N_DP * CSAMP, VSAMP))
    return jnp.stack(results, axis=0)
```

```python
import functools
import math

import jax
import jax.numpy as jnp
from jax import lax
from jax.experimental import pallas as pl
from jax.experimental.pallas import tpu as pltpu
from jax.sharding import PartitionSpec as P

D = 8192
FF = 28672
ROUNDS = 2
TOK = 256
W = 128
NX = 4
NG = 14
NS = 2 * NX + 3 * NG
STEPS = (NS + 2) // 3
MESH = pl.DeviceIdType.MESH
F32 = jnp.float32
BF16 = jnp.bfloat16


def derive(gate, up, grad):
    sig = jax.nn.sigmoid(gate)
    act = gate * sig
    hidden = (act * up).astype(BF16)
    grad_gate = (grad * up * sig * (1.0 + gate * (1.0 - sig))).astype(BF16)
    grad_up = (grad * act).astype(BF16)
    return hidden, grad_gate, grad_up


def lanes(block):
    return pl.ds(pl.multiple_of(block * W, W), W)


def spread_kernel(
    owner_chip,
    core_ref,
    cg, cu, cd, cx, cy,
    vg, vu, vd, vx, vy,
    out_ref,
    rg, ru, rd, rx, ry,
    sg, su, sd, sx, sy,
    cand, val, acc,
    load_sem, stage_sem, swap_send, swap_recv,
    recv_sem, sib_recv, sib_send, send_sem, ack,
):
    dp = lax.axis_index("dp")
    t = lax.axis_index("tensor")
    core = dp % 2
    x = (dp // 2) % 4
    yh = dp // 8
    ox, oy = owner_chip % 4, owner_chip // 4
    bits = ((x // 2 + x % 2) % 2, x // 2, yh)
    obits = ((ox // 2 + ox % 2) % 2, ox // 2, oy)
    r = [(b + o) % 2 for b, o in zip(bits, obits)]
    nbr = [
        (yh * 8 + (x + 1 - 2 * (x % 2)) * 2 + core, t),
        (yh * 8 + (3 - x) * 2 + core, t),
        ((1 - yh) * 8 + x * 2 + core, t),
    ]
    sib = (yh * 8 + x * 2 + 1 - core, t)
    level = r[0] + r[1] + r[2]
    is_root = level == 0

    loads = [
        pltpu.make_async_copy(a, b, load_sem.at[i])
        for i, (a, b) in enumerate(((cx, rx), (cy, ry), (cg, rg), (cu, ru), (cd, rd)))
    ]
    for c in loads:
        c.start()

    def half(ref, home, n):
        return ref.at[:, pl.ds(pl.multiple_of(home * (n * W), W), n * W)]

    raw = ((vx, sx, NX), (vy, sy, NX), (vg, sg, NG), (vu, su, NG), (vd, sd, NG))
    stage = [
        pltpu.make_async_copy(half(a, core, n), b.at[0], stage_sem.at[i])
        for i, (a, b, n) in enumerate(raw)
    ]
    swap = [
        pltpu.make_async_remote_copy(
            half(a, 1 - core, n), b.at[1], swap_send.at[i], swap_recv.at[i],
            device_id=sib, device_id_type=MESH,
        )
        for i, (a, b, n) in enumerate(raw)
    ]

    @pl.when(is_root)
    def _():
        for c in stage:
            c.start()

    barrier = pltpu.get_barrier_semaphore()
    for n in nbr + [sib]:
        pl.semaphore_signal(barrier, inc=1, device_id=n, device_id_type=MESH)
    pl.semaphore_wait(barrier, 4)

    @pl.when(is_root)
    def _():
        for c in swap:
            c.start()

    for n in nbr + [sib]:
        pl.semaphore_signal(ack, inc=1, device_id=n, device_id_type=MESH)

    base = core * NS
    obase = (1 - core) * NS
    mine = jnp.where(core_ref[0] == core, 1.0, 0.0).astype(F32)

    def pick(ref, block):
        own = ref[0, :, lanes(block)].astype(F32)
        other = ref[1, :, lanes(block)].astype(F32)
        return own * mine + other * (1.0 - mine)

    def derive_val(k):
        h, g, u = derive(pick(sg, k), pick(su, k), pick(sd, k))
        val[base + 2 * NX + 3 * k] = h
        val[base + 2 * NX + 3 * k + 1] = g
        val[base + 2 * NX + 3 * k + 2] = u

    @pl.when(is_root)
    def _():
        for c in stage:
            c.wait()
        for c in swap:
            c.wait_recv()
        for k in range(NX):
            val[base + k] = pick(sx, k).astype(BF16)
            val[base + NX + k] = pick(sy, k).astype(BF16)

    acc[...] = jnp.zeros_like(acc)

    def derive_cand(b, home, k):
        q = home * NG + k
        h, g, u = derive(
            rg[:, lanes(q)].astype(F32), ru[:, lanes(q)].astype(F32), rd[:, lanes(q)].astype(F32)
        )
        cand[b + 2 * NX + 3 * k] = h
        cand[b + 2 * NX + 3 * k + 1] = g
        cand[b + 2 * NX + 3 * k + 2] = u

    for c in loads:
        c.wait()
    for b, home in ((base, core), (obase, 1 - core)):
        for k in range(NX):
            cand[b + k] = rx[:, lanes(home * NX + k)]
            cand[b + NX + k] = ry[:, lanes(home * NX + k)]

    def remote(s, way, slot):
        return pltpu.make_async_remote_copy(
            val.at[base + s], val.at[base + s], send_sem.at[slot, s], recv_sem.at[s],
            device_id=nbr[way], device_id_type=MESH,
        )

    def to_sib(s):
        return pltpu.make_async_remote_copy(
            val.at[base + s], val.at[base + s], sib_send.at[s], sib_recv.at[s],
            device_id=sib, device_id_type=MESH,
        )

    def roles(j):
        a, b, c = r[j], r[(j + 2) % 3], r[(j + 1) % 3]
        first = jnp.where(is_root, 1, a * jnp.minimum(b + c, 1))
        second = a * (1 - b)
        third = a * (1 - b) * (1 - c)
        depth = jnp.where(is_root, 0, level + 2 * (1 - a))
        return first, second, third, depth

    role = [roles(j) for j in range(3)]
    ways = [(j, (j + 2) % 3, (j + 1) % 3) for j in range(3)]

    def multiply(b, s):
        kind = jnp.where(s < NX, 0, jnp.where(s < 2 * NX, 1, jnp.where((s - 2 * NX) % 3 == 0, 3, 2)))
        acc[kind] += lax.dot_general(
            cand[b + s], val[b + s], (((1,), (1,)), ((), ())), preferred_element_type=F32
        )

    def at(tau, j):
        step = tau - role[j][3]
        s = 3 * step + j
        return s, (step >= 0) & (s < NS)

    def body(tau, carry):
        for j in range(3):
            s, ok = at(tau, j)

            @pl.when(ok)
            def _(s=s, j=j):
                @pl.when(level > 0)
                def _():
                    remote(s, j, 0).wait_recv()

                for slot in range(3):
                    @pl.when(role[j][slot] == 1)
                    def _(slot=slot):
                        remote(s, ways[j][slot], slot).start()

                to_sib(s).start()

        @pl.when((tau >= 1) & (tau < NG + 1))
        def _():
            @pl.when(is_root)
            def _():
                derive_val(tau - 1)

            derive_cand(base, core, tau - 1)
            derive_cand(obase, 1 - core, tau - 1)

        for j in range(3):
            s, ok = at(tau, j)

            @pl.when(ok)
            def _(s=s):
                multiply(base, s)

        for j in range(3):
            s, ok = at(tau - 1, j)

            @pl.when(ok)
            def _(s=s):
                to_sib(s).wait_recv()
                multiply(obase, s)

        return carry

    lax.fori_loop(0, STEPS + 5, body, 0)
    out_ref[...] = acc[...].astype(BF16)

    def finish(step, carry):
        for j in range(3):
            s = 3 * step + j

            @pl.when(s < NS)
            def _(s=s, j=j):
                for slot in range(3):
                    @pl.when(role[j][slot] == 1)
                    def _(slot=slot):
                        remote(s, ways[j][slot], slot).wait_send()

                to_sib(s).wait_send()

        return carry

    lax.fori_loop(0, STEPS, finish, 0)

    @pl.when(is_root)
    def _():
        for c in swap:
            c.wait_send()

    pl.semaphore_wait(ack, 4)


def spread(owner_chip, core, *arrays):
    any_spec = pl.BlockSpec(memory_space=pl.ANY)
    return pl.pallas_call(
        functools.partial(spread_kernel, owner_chip),
        out_shape=jax.ShapeDtypeStruct((4, TOK, TOK), BF16),
        in_specs=[pl.BlockSpec(memory_space=pltpu.SMEM)] + [any_spec] * 10,
        out_specs=pl.BlockSpec(memory_space=pltpu.VMEM),
        scratch_shapes=[pltpu.VMEM((TOK, 2 * NG * W), BF16)] * 3
        + [pltpu.VMEM((TOK, 2 * NX * W), BF16)] * 2
        + [pltpu.VMEM((2, TOK, NG * W), BF16)] * 3
        + [pltpu.VMEM((2, TOK, NX * W), BF16)] * 2
        + [
            pltpu.VMEM((2 * NS, TOK, W), BF16),
            pltpu.VMEM((2 * NS, TOK, W), BF16),
            pltpu.VMEM((4, TOK, TOK), F32),
            pltpu.SemaphoreType.DMA((5,)),
            pltpu.SemaphoreType.DMA((5,)),
            pltpu.SemaphoreType.DMA((5,)),
            pltpu.SemaphoreType.DMA((5,)),
            pltpu.SemaphoreType.DMA((NS,)),
            pltpu.SemaphoreType.DMA((NS,)),
            pltpu.SemaphoreType.DMA((NS,)),
            pltpu.SemaphoreType.DMA((3, NS)),
            pltpu.SemaphoreType.REGULAR,
        ],
        compiler_params=pltpu.CompilerParams(
            collective_id=owner_chip, has_side_effects=True, vmem_limit_bytes=56 * 2**20
        ),
        name="spread",
    )(core, *arrays)


def reduce_kernel(
    gram0, gram1, cand_len, val_len, owner, out_ref,
    slabs, parts, send_sem, recv_sem, part_send, part_recv,
):
    dp = lax.axis_index("dp")
    t = lax.axis_index("tensor")
    rows = TOK // 8
    peers = [(t + k) % 8 for k in range(1, 8)]
    barrier = pltpu.get_barrier_semaphore()
    for p in peers:
        pl.semaphore_signal(barrier, inc=1, device_id=(dp, p), device_id_type=MESH)
    pl.semaphore_wait(barrier, 7)

    def slab(ref, p):
        return ref.at[:, pl.ds(pl.multiple_of(p * rows, rows), rows), :]

    copies = []
    for rnd, gram in enumerate((gram0, gram1)):
        for k, p in enumerate(peers):
            c = pltpu.make_async_remote_copy(
                slab(gram, p), slabs.at[k, rnd], send_sem.at[rnd, k], recv_sem.at[rnd, k],
                device_id=(dp, p), device_id_type=MESH,
            )
            c.start()
            copies.append(c)

    token = lax.broadcasted_iota(jnp.int32, (8, rows), 1) + t * rows
    label = lax.broadcasted_iota(jnp.int32, (8, rows), 0)
    cand_hot = jnp.zeros((8, rows), F32)
    row8 = lax.broadcasted_iota(jnp.int32, (8, 128), 0)
    col8 = lax.broadcasted_iota(jnp.int32, (8, 128), 1)
    n_rows = jnp.ones((8, 128), F32)
    start = jnp.int32(0)
    for i in range(8):
        n = cand_len[0, i]
        inside = (label == i) & (token >= start) & (token < start + n)
        cand_hot = jnp.where(inside, 1.0, cand_hot)
        n_rows = jnp.where(row8 == i, n.astype(F32), n_rows)
        start = start + n

    vtok = lax.broadcasted_iota(jnp.int32, (128, TOK), 1)
    vlab = lax.broadcasted_iota(jnp.int32, (128, TOK), 0)
    hots, norms = [], []
    for rnd in range(ROUNDS):
        hot = jnp.zeros((128, TOK), F32)
        m_cols = jnp.ones((8, 128), F32)
        start = jnp.int32(0)
        for i in range(8):
            m = val_len[owner[rnd], i]
            inside = (vlab == i) & (vtok >= start) & (vtok < start + m)
            hot = jnp.where(inside, 1.0, hot)
            m_cols = jnp.where(col8 == i, m.astype(F32), m_cols)
            start = start + m
        hots.append(hot)
        norms.append((1.0 / math.sqrt(D * FF)) / jnp.sqrt(n_rows * m_cols))

    for rnd, gram in enumerate((gram0, gram1)):
        total = gram[:, pl.ds(pl.multiple_of(t * rows, rows), rows), :].astype(F32)
        for k in range(7):
            copies[rnd * 7 + k].wait_recv()
            total = total + slabs[k, rnd].astype(F32)
        pair = total[0] * total[2] + total[3] * total[1]
        cols = lax.dot_general(
            pair, hots[rnd], (((1,), (1,)), ((), ())),
            precision=lax.Precision.HIGHEST, preferred_element_type=F32,
        )
        parts[t, rnd] = jnp.dot(
            cand_hot, cols, precision=lax.Precision.HIGHEST, preferred_element_type=F32
        )

    sums = []
    for k, p in enumerate(peers):
        c = pltpu.make_async_remote_copy(
            parts.at[t], parts.at[t], part_send.at[k], part_recv.at[k],
            device_id=(dp, p), device_id_type=MESH,
        )
        c.start()
        sums.append(c)
    for c in sums:
        c.wait_recv()
    for rnd in range(ROUNDS):
        total = parts[0, rnd]
        for k in range(1, 8):
            total = total + parts[k, rnd]
        out_ref[rnd] = (total * norms[rnd])[:, :8]
    for c in copies + sums:
        c.wait_send()


def reduce(gram0, gram1, cand_len, val_len, owner):
    smem = pl.BlockSpec(memory_space=pltpu.SMEM)
    vmem = pl.BlockSpec(memory_space=pltpu.VMEM)
    return pl.pallas_call(
        reduce_kernel,
        out_shape=jax.ShapeDtypeStruct((ROUNDS, 8, 8), F32),
        in_specs=[vmem, vmem, smem, smem, smem],
        out_specs=vmem,
        scratch_shapes=[
            pltpu.VMEM((7, ROUNDS, 4, TOK // 8, TOK), BF16),
            pltpu.VMEM((8, ROUNDS, 8, 128), F32),
            pltpu.SemaphoreType.DMA((ROUNDS, 7)),
            pltpu.SemaphoreType.DMA((ROUNDS, 7)),
            pltpu.SemaphoreType.DMA((7,)),
            pltpu.SemaphoreType.DMA((7,)),
        ],
        compiler_params=pltpu.CompilerParams(
            collective_id=8, has_side_effects=True, vmem_limit_bytes=32 * 2**20
        ),
        name="reduce",
    )(gram0, gram1, cand_len, val_len, owner)


def local(*args):
    arrays = args[:10]
    cand_len, val_len, owner = args[10:]
    branches = [functools.partial(spread, chip) for chip in range(8)]
    grams = []
    for rnd in range(ROUNDS):
        o = owner[rnd]
        grams.append(lax.switch(o // 2, branches, (o % 2).reshape(1), *arrays))
    return reduce(*grams, cand_len, val_len, owner)


def solution(mesh):
    tile = P("dp", "tensor")
    in_specs = (tile,) * 10 + (P("dp", None), P(), P())
    return jax.shard_map(
        local, mesh=mesh, in_specs=in_specs, out_specs=P(None, "dp", None), check_vma=False
    )
```

```python
import functools
import math

import jax
import jax.numpy as jnp
from jax import lax
from jax.experimental import pallas as pl
from jax.experimental.pallas import tpu as pltpu
from jax.sharding import PartitionSpec as P

D = 8192
FF = 28672
ROUNDS = 2
TOK = 256
ROWS = TOK // 8
W = 128
NX = 4
NG = 14
NS = 2 * NX + 3 * NG
STEPS = (NS + 2) // 3
SKEW = 3
SLAG = 2
OFFS = 5
EARLY_STEP = (2 * NX + NG - 1) // 3
LATE_STEP = STEPS - 1
MESH = pl.DeviceIdType.MESH
F32 = jnp.float32
BF16 = jnp.bfloat16


def derive(gate, up, grad):
    sig = jax.nn.sigmoid(gate)
    act = gate * sig
    hidden = (act * up).astype(BF16)
    grad_gate = (grad * up * sig * (1.0 + gate * (1.0 - sig))).astype(BF16)
    grad_up = (grad * act).astype(BF16)
    return hidden, grad_gate, grad_up


def lanes(block):
    return pl.ds(pl.multiple_of(block * W, W), W)


def rows_of(p):
    return pl.ds(pl.multiple_of(p * ROWS, ROWS), ROWS)


def kernel(
    chips,
    meta, cand_len, val_len,
    cg, cu, cd, cx, cy,
    vg, vu, vd, vx, vy,
    out_ref,
    rg, ru, rd, rx, ry,
    sg, su, sd, sx, sy,
    cand, val, acc, gram, slabs, parts,
    load_sem, stage_sem, swap_send, swap_recv,
    recv_sem, sib_recv, sib_send, send_sem,
    gram_send, gram_recv, part_send, part_recv,
):
    dp = lax.axis_index("dp")
    t = lax.axis_index("tensor")
    core = dp % 2
    x = (dp // 2) % 4
    yh = dp // 8
    bits = ((x // 2 + x % 2) % 2, x // 2, yh)
    nbr = [
        (yh * 8 + (x + 1 - 2 * (x % 2)) * 2 + core, t),
        (yh * 8 + (3 - x) * 2 + core, t),
        ((1 - yh) * 8 + x * 2 + core, t),
    ]
    sib = (yh * 8 + x * 2 + 1 - core, t)
    peers = [(dp, (t + k) % 8) for k in range(1, 8)]
    base = core * NS
    obase = (1 - core) * NS

    levels, roles = [], []
    for chip in chips:
        ox, oy = chip % 4, chip // 4
        obits = ((ox // 2 + ox % 2) % 2, ox // 2, oy)
        r = [(b + o) % 2 for b, o in zip(bits, obits)]
        level = r[0] + r[1] + r[2]
        levels.append(level)
        tree = []
        for j in range(3):
            a, b, c = r[j], r[(j + 2) % 3], r[(j + 1) % 3]
            first = jnp.where(level == 0, 1, a * jnp.minimum(b + c, 1))
            second = a * (1 - b)
            third = a * (1 - b) * (1 - c)
            depth = jnp.where(level == 0, 0, level + 2 * (1 - a))
            tree.append((first, second, third, depth))
        roles.append(tree)
    any_root = levels[0] * levels[1] == 0
    ways = [(j, (j + 2) % 3, (j + 1) % 3) for j in range(3)]

    def half(ref, home, n):
        return ref.at[:, pl.ds(pl.multiple_of(home * (n * W), W), n * W)]

    raw = ((vx, sx, NX), (vy, sy, NX), (vg, sg, NG), (vu, su, NG), (vd, sd, NG))
    stage = [
        pltpu.make_async_copy(half(a, core, n), b.at[0], stage_sem.at[i])
        for i, (a, b, n) in enumerate(raw)
    ]
    swap = [
        pltpu.make_async_remote_copy(
            half(a, 1 - core, n), b.at[1], swap_send.at[i], swap_recv.at[i],
            device_id=sib, device_id_type=MESH,
        )
        for i, (a, b, n) in enumerate(raw)
    ]
    loads = [
        pltpu.make_async_copy(a, b, load_sem.at[i])
        for i, (a, b) in enumerate(((cx, rx), (cy, ry), (cg, rg), (cu, ru), (cd, rd)))
    ]

    @pl.when(any_root)
    def _():
        for c in stage:
            c.start()

    for c in loads:
        c.start()

    barrier = pltpu.get_barrier_semaphore()
    for n in nbr + [sib] + peers:
        pl.semaphore_signal(barrier, inc=1, device_id=n, device_id_type=MESH)
    pl.semaphore_wait(barrier, 11)

    @pl.when(any_root)
    def _():
        for c in swap:
            c.start()

    acc[...] = jnp.zeros_like(acc)
    mine = [jnp.where(meta[rnd] % 2 == core, 1.0, 0.0).astype(F32) for rnd in range(ROUNDS)]

    def pick(rnd, ref, block):
        own = ref[0, :, lanes(block)].astype(F32)
        other = ref[1, :, lanes(block)].astype(F32)
        return own * mine[rnd] + other * (1.0 - mine[rnd])

    def put(ref, index, b, k, blocks):
        h, g, u = blocks
        ref[index + b + 2 * NX + k] = h
        ref[index + b + 2 * NX + NG + 2 * k] = g
        ref[index + b + 2 * NX + NG + 2 * k + 1] = u

    def derive_val(rnd, k):
        blocks = derive(pick(rnd, sg, k), pick(rnd, su, k), pick(rnd, sd, k))
        put(val, rnd * 2 * NS, base, k, blocks)

    def derive_cand(b, home, k):
        q = lanes(home * NG + k)
        put(cand, 0, b, k, derive(rg[:, q].astype(F32), ru[:, q].astype(F32), rd[:, q].astype(F32)))

    @pl.when(any_root)
    def _():
        for i in range(2):
            stage[i].wait()
            swap[i].wait_recv()

    for rnd in range(ROUNDS):
        @pl.when(levels[rnd] == 0)
        def _(rnd=rnd):
            for k in range(NX):
                val[rnd * 2 * NS + base + k] = pick(rnd, sx, k).astype(BF16)
                val[rnd * 2 * NS + base + NX + k] = pick(rnd, sy, k).astype(BF16)

    def remote(rnd, s, way, slot):
        ref = val.at[rnd * 2 * NS + base + s]
        return pltpu.make_async_remote_copy(
            ref, ref, send_sem.at[rnd, slot, s], recv_sem.at[rnd, s],
            device_id=nbr[way], device_id_type=MESH,
        )

    def to_sib(rnd, s):
        ref = val.at[rnd * 2 * NS + base + s]
        return pltpu.make_async_remote_copy(
            ref, ref, sib_send.at[rnd, s], sib_recv.at[rnd, s],
            device_id=sib, device_id_type=MESH,
        )

    def from_sib(rnd, s):
        ref = val.at[rnd * 2 * NS + obase + s]
        return pltpu.make_async_remote_copy(
            ref, ref, sib_send.at[rnd, s], sib_recv.at[rnd, s],
            device_id=sib, device_id_type=MESH,
        )

    def exchange(rnd, part):
        tiles = pl.ds(0, 3) if part == 0 else pl.ds(3, 1)
        return [
            pltpu.make_async_remote_copy(
                gram.at[rnd, tiles, rows_of(p[1])], slabs.at[k, rnd, tiles],
                gram_send.at[rnd, part, k], gram_recv.at[rnd, part, k],
                device_id=p, device_id_type=MESH,
            )
            for k, p in enumerate(peers)
        ]

    def send_gram(rnd, part):
        tiles = range(3) if part == 0 else range(3, 4)
        for i in tiles:
            gram[rnd, i] = acc[rnd, i].astype(BF16)
        for c in exchange(rnd, part):
            c.start()

    def multiply(i, tau):
        side, rnd, j = i // 6, (i // 3) % 2, i % 3
        depth = 0
        for q in range(ROUNDS):
            for p in range(3):
                depth = jnp.where((rnd == q) & (j == p), roles[q][p][3], depth)
        step = tau - OFFS * rnd - SKEW * depth - SLAG * side
        s = 3 * step + j

        @pl.when((step >= 0) & (s < NS))
        def _():
            @pl.when(side == 1)
            def _():
                from_sib(rnd, s).wait_recv()

            b = jnp.where(side == 0, base, obase)
            kind = jnp.where(
                s < NX, 0, jnp.where(s < 2 * NX, 1, jnp.where(s < 2 * NX + NG, 2, 3))
            )
            acc[rnd, kind] += lax.dot_general(
                cand[b + s], val[rnd * 2 * NS + b + s], (((1,), (1,)), ((), ())),
                preferred_element_type=F32,
            )

    def body(tau, carry):
        for rnd in range(ROUNDS):
            for j in range(3):
                step = tau - OFFS * rnd - SKEW * roles[rnd][j][3]
                s = 3 * step + j

                @pl.when((step >= 0) & (s < NS))
                def _(rnd=rnd, s=s, j=j):
                    @pl.when(levels[rnd] > 0)
                    def _():
                        remote(rnd, s, j, 0).wait_recv()

                    for slot in range(3):
                        @pl.when(roles[rnd][j][slot] == 1)
                        def _(slot=slot):
                            remote(rnd, s, ways[j][slot], slot).start()

                    to_sib(rnd, s).start()

        @pl.when(tau == 0)
        def _():
            for c in loads:
                c.wait()
            for b, home in ((base, core), (obase, 1 - core)):
                for k in range(NX):
                    cand[b + k] = rx[:, lanes(home * NX + k)]
                    cand[b + NX + k] = ry[:, lanes(home * NX + k)]

            @pl.when(any_root)
            def _():
                for i in range(2, 5):
                    stage[i].wait()
                    swap[i].wait_recv()

        def derive_one(k, carry):
            for rnd in range(ROUNDS):
                @pl.when(levels[rnd] == 0)
                def _(rnd=rnd):
                    derive_val(rnd, k)

            derive_cand(base, core, k)
            derive_cand(obase, 1 - core, k)
            return carry

        lax.fori_loop(
            jnp.clip(3 * tau - 5, 0, NG), jnp.clip(3 * tau - 2, 0, NG), derive_one, 0
        )

        def multiply_one(i, carry):
            multiply(i, tau)
            return carry

        lax.fori_loop(0, 12, multiply_one, 0)

        for rnd, part in ((0, 0), (0, 1), (1, 0)):
            turn = OFFS * rnd + (EARLY_STEP, LATE_STEP)[part] + 4 * SKEW + SLAG

            @pl.when(tau == turn)
            def _(rnd=rnd, part=part):
                send_gram(rnd, part)

        return carry

    lax.fori_loop(0, OFFS + STEPS + 4 * SKEW + SLAG, body, 0)
    send_gram(1, 1)

    token = lax.broadcasted_iota(jnp.int32, (8, ROWS), 1) + t * ROWS
    label = lax.broadcasted_iota(jnp.int32, (8, ROWS), 0)
    row8 = lax.broadcasted_iota(jnp.int32, (8, 128), 0)
    col8 = lax.broadcasted_iota(jnp.int32, (8, 128), 1)
    vtok = lax.broadcasted_iota(jnp.int32, (128, TOK), 1)
    vlab = lax.broadcasted_iota(jnp.int32, (128, TOK), 0)
    cand_hot = jnp.zeros((8, ROWS), F32)
    n_rows = jnp.ones((8, 128), F32)
    start = jnp.int32(0)
    for i in range(8):
        n = cand_len[0, i]
        inside = (label == i) & (token >= start) & (token < start + n)
        cand_hot = jnp.where(inside, 1.0, cand_hot)
        n_rows = jnp.where(row8 == i, n.astype(F32), n_rows)
        start = start + n

    norms = []
    for rnd in range(ROUNDS):
        hot = jnp.zeros((128, TOK), F32)
        m_cols = jnp.ones((8, 128), F32)
        start = jnp.int32(0)
        for i in range(8):
            m = val_len[meta[rnd], i]
            inside = (vlab == i) & (vtok >= start) & (vtok < start + m)
            hot = jnp.where(inside, 1.0, hot)
            m_cols = jnp.where(col8 == i, m.astype(F32), m_cols)
            start = start + m
        norms.append((1.0 / math.sqrt(D * FF)) / jnp.sqrt(n_rows * m_cols))
        for part in range(2):
            for c in exchange(rnd, part):
                c.wait_recv()
        total = acc[rnd, :, rows_of(t), :]
        for k in range(7):
            total = total + slabs[k, rnd].astype(F32)
        pair = total[0] * total[3] + total[2] * total[1]
        cols = lax.dot_general(
            pair, hot, (((1,), (1,)), ((), ())),
            precision=lax.Precision.HIGHEST, preferred_element_type=F32,
        )
        parts[t, rnd] = jnp.dot(
            cand_hot, cols, precision=lax.Precision.HIGHEST, preferred_element_type=F32
        )

    sums = [
        pltpu.make_async_remote_copy(
            parts.at[t], parts.at[t], part_send.at[k], part_recv.at[k],
            device_id=p, device_id_type=MESH,
        )
        for k, p in enumerate(peers)
    ]
    for c in sums:
        c.start()

    def finish(step, carry):
        for rnd in range(ROUNDS):
            for j in range(3):
                s = 3 * step + j

                @pl.when(s < NS)
                def _(rnd=rnd, s=s, j=j):
                    for slot in range(3):
                        @pl.when(roles[rnd][j][slot] == 1)
                        def _(slot=slot):
                            remote(rnd, s, ways[j][slot], slot).wait_send()

                    to_sib(rnd, s).wait_send()

        return carry

    lax.fori_loop(0, STEPS, finish, 0)

    @pl.when(any_root)
    def _():
        for c in swap:
            c.wait_send()

    for rnd in range(ROUNDS):
        for part in range(2):
            for c in exchange(rnd, part):
                c.wait_send()

    for k in range(1, 8):
        pltpu.make_async_remote_copy(
            parts.at[t], parts.at[(t + 8 - k) % 8], part_send.at[k - 1], part_recv.at[k - 1],
            device_id=peers[k - 1], device_id_type=MESH,
        ).wait_recv()
    scores = []
    for rnd in range(ROUNDS):
        total = parts[0, rnd]
        for k in range(1, 8):
            total = total + parts[k, rnd]
        scores.append((total * norms[rnd])[:, :8])
    swapped = jnp.full((8, 8), meta[2], jnp.int32) == 1
    out_ref[0] = jnp.where(swapped, scores[1], scores[0])
    out_ref[1] = jnp.where(swapped, scores[0], scores[1])
    for c in sums:
        c.wait_send()


def spread(number, chips, meta, cand_len, val_len, *arrays):
    any_spec = pl.BlockSpec(memory_space=pl.ANY)
    smem = pl.BlockSpec(memory_space=pltpu.SMEM)
    return pl.pallas_call(
        functools.partial(kernel, chips),
        out_shape=jax.ShapeDtypeStruct((ROUNDS, 8, 8), F32),
        in_specs=[smem] * 3 + [any_spec] * 10,
        out_specs=pl.BlockSpec(memory_space=pltpu.VMEM),
        scratch_shapes=[pltpu.VMEM((TOK, 2 * NG * W), BF16)] * 3
        + [pltpu.VMEM((TOK, 2 * NX * W), BF16)] * 2
        + [pltpu.VMEM((2, TOK, NG * W), BF16)] * 3
        + [pltpu.VMEM((2, TOK, NX * W), BF16)] * 2
        + [
            pltpu.VMEM((2 * NS, TOK, W), BF16),
            pltpu.VMEM((ROUNDS * 2 * NS, TOK, W), BF16),
            pltpu.VMEM((ROUNDS, 4, TOK, TOK), F32),
            pltpu.VMEM((ROUNDS, 4, TOK, TOK), BF16),
            pltpu.VMEM((7, ROUNDS, 4, ROWS, TOK), BF16),
            pltpu.VMEM((8, ROUNDS, 8, 128), F32),
            pltpu.SemaphoreType.DMA((5,)),
            pltpu.SemaphoreType.DMA((5,)),
            pltpu.SemaphoreType.DMA((5,)),
            pltpu.SemaphoreType.DMA((5,)),
            pltpu.SemaphoreType.DMA((ROUNDS, NS)),
            pltpu.SemaphoreType.DMA((ROUNDS, NS)),
            pltpu.SemaphoreType.DMA((ROUNDS, NS)),
            pltpu.SemaphoreType.DMA((ROUNDS, 3, NS)),
            pltpu.SemaphoreType.DMA((ROUNDS, 2, 7)),
            pltpu.SemaphoreType.DMA((ROUNDS, 2, 7)),
            pltpu.SemaphoreType.DMA((7,)),
            pltpu.SemaphoreType.DMA((7,)),
        ],
        compiler_params=pltpu.CompilerParams(
            collective_id=number, has_side_effects=True, vmem_limit_bytes=56 * 2**20
        ),
        name="spread",
    )(meta, cand_len, val_len, *arrays)


PAIRS = [(a, b) for a in range(8) for b in range(a, 8)]


def local(*args):
    arrays = args[:10]
    cand_len, val_len, owner = args[10:]
    low, high = jnp.minimum(owner[0], owner[1]), jnp.maximum(owner[0], owner[1])
    meta = jnp.stack([low, high, (owner[0] > owner[1]).astype(jnp.int32)])
    a, b = low >> 1, high >> 1
    index = 8 * a - ((a * (a - 1)) >> 1) + b - a
    branches = [functools.partial(spread, i, chips) for i, chips in enumerate(PAIRS)]
    return lax.switch(index, branches, meta, cand_len, val_len, *arrays)


def solution(mesh):
    tile = P("dp", "tensor")
    in_specs = (tile,) * 10 + (P("dp", None), P(), P())
    return jax.shard_map(
        local, mesh=mesh, in_specs=in_specs, out_specs=P(None, "dp", None), check_vma=False
    )
```

```python
import functools
import math

import jax
import jax.numpy as jnp
from jax import lax
from jax.experimental import pallas as pl
from jax.experimental.pallas import tpu as pltpu
from jax.sharding import PartitionSpec as P

D = 8192
FF = 28672
ROUNDS = 2
TOK = 256
ROWS = TOK // 8
W = 128
NX = 4
NG = 14
NS = 2 * NX + 3 * NG
STEPS = (NS + 2) // 3
SKEW = 3
GROUP = 4
SLAG = GROUP + 1
OFFS = 3
CHUNK = 256
TILE_STEPS = ((NX - 1) // 3, (2 * NX - 1) // 3, (2 * NX + NG - 1) // 3, STEPS - 1)
MESH = pl.DeviceIdType.MESH
F32 = jnp.float32
BF16 = jnp.bfloat16


def derive(gate, up, grad):
    sig = jax.nn.sigmoid(gate)
    act = gate * sig
    hidden = (act * up).astype(BF16)
    grad_gate = (grad * up * sig * (1.0 + gate * (1.0 - sig))).astype(BF16)
    grad_up = (grad * act).astype(BF16)
    return hidden, grad_gate, grad_up


def lanes(block):
    return pl.ds(pl.multiple_of(block * W, W), W)


def rows_of(p):
    return pl.ds(pl.multiple_of(p * ROWS, ROWS), ROWS)


def slot_of(s):
    return STEPS * (s % 3) + s // 3


def loop(count, function):
    def step(i, carry):
        function(i)
        return carry

    lax.fori_loop(0, count, step, 0)


def kernel(
    chips,
    meta, cand_len, val_len,
    cg, cu, cd, cx, cy,
    vg, vu, vd, vx, vy,
    out_ref,
    rg, ru, rd, rx, ry,
    sg, su, sd, sx, sy,
    cand, val, acc, gram, slabs, parts, norm,
    load_sem, stage_sem, swap_send, swap_recv,
    recv_sem, sib_recv, sib_send, send_sem,
    gram_send, gram_recv, part_send, part_recv,
):
    dp = lax.axis_index("dp")
    t = lax.axis_index("tensor")
    core = dp % 2
    x = (dp // 2) % 4
    yh = dp // 8
    bits = ((x // 2 + x % 2) % 2, x // 2, yh)
    nbr = [
        yh * 8 + (x + 1 - 2 * (x % 2)) * 2 + core,
        yh * 8 + (3 - x) * 2 + core,
        (1 - yh) * 8 + x * 2 + core,
    ]
    sib = (yh * 8 + x * 2 + 1 - core, t)
    base = core * NS
    obase = (1 - core) * NS

    places = []
    for chip in chips:
        ox, oy = chip % 4, chip // 4
        obits = ((ox // 2 + ox % 2) % 2, ox // 2, oy)
        places.append([(b + o) % 2 for b, o in zip(bits, obits)])
    any_root = (places[0][0] + places[0][1] + places[0][2]) * (
        places[1][0] + places[1][1] + places[1][2]
    ) == 0

    def place(rnd):
        return [jnp.where(rnd == 0, p, q) for p, q in zip(*places)]

    def depth_at(level, a):
        return jnp.where(level == 0, 0, level + 2 - 2 * a)

    def half(ref, home, n):
        return ref.at[:, pl.ds(pl.multiple_of(home * (n * W), W), n * W)]

    raw = ((vx, sx, NX), (vy, sy, NX), (vg, sg, NG), (vu, su, NG), (vd, sd, NG))
    stage = [
        pltpu.make_async_copy(half(a, core, n), b.at[0], stage_sem.at[i])
        for i, (a, b, n) in enumerate(raw)
    ]
    swap = [
        pltpu.make_async_remote_copy(
            half(a, 1 - core, n), b.at[1], swap_send.at[i], swap_recv.at[i],
            device_id=sib, device_id_type=MESH,
        )
        for i, (a, b, n) in enumerate(raw)
    ]
    loads = [
        pltpu.make_async_copy(a, b, load_sem.at[i])
        for i, (a, b) in enumerate(((cx, rx), (cy, ry), (cg, rg), (cu, ru), (cd, rd)))
    ]

    @pl.when(any_root)
    def _():
        for c in stage:
            c.start()

    for c in loads:
        c.start()

    def signal(n):
        pl.semaphore_signal(barrier, inc=1, device_id=n, device_id_type=MESH)

    barrier = pltpu.get_barrier_semaphore()
    for n in nbr:
        signal((n, t))
    signal(sib)
    loop(7, lambda k: signal((dp, (t + k + 1) % 8)))

    def clear(i):
        acc[i // 4, i % 4] = jnp.zeros((TOK, TOK), F32)

    loop(8, clear)
    pl.semaphore_wait(barrier, 11)

    @pl.when(any_root)
    def _():
        for c in swap:
            c.start()

    def mine(rnd):
        return jnp.where(meta[rnd] % 2 == core, 1.0, 0.0).astype(F32)

    def pick(m, ref, rows, cols):
        own = ref[0, rows, cols].astype(F32)
        other = ref[1, rows, cols].astype(F32)
        return own * m + other * (1.0 - m)

    def put(ref, first, k, rows, blocks):
        h, g, u = blocks
        ref[first + slot_of(2 * NX + k), rows, :] = h
        ref[first + slot_of(2 * NX + NG + 2 * k), rows, :] = g
        ref[first + slot_of(2 * NX + NG + 2 * k + 1), rows, :] = u

    def chunk(i):
        return pl.ds(pl.multiple_of(i * CHUNK, CHUNK), CHUNK)

    def derive_val(rnd, k):
        m = mine(rnd)

        def one(i):
            rows, cols = chunk(i), lanes(k)
            blocks = derive(*(pick(m, ref, rows, cols) for ref in (sg, su, sd)))
            put(val, rnd * 2 * NS + base, k, rows, blocks)

        loop(TOK // CHUNK, one)

    def derive_cand(home, k):
        def one(i):
            rows, cols = chunk(i), lanes(home * NG + k)
            blocks = derive(*(ref[rows, cols].astype(F32) for ref in (rg, ru, rd)))
            put(cand, home * NS, k, rows, blocks)

        loop(TOK // CHUNK, one)

    def first_blocks(rnd):
        m = mine(rnd)

        @pl.when(sum(place(rnd)) == 0)
        def _():
            def one(k):
                first = rnd * 2 * NS + base
                val[first + slot_of(k)] = pick(m, sx, slice(None), lanes(k)).astype(BF16)
                val[first + slot_of(NX + k)] = pick(m, sy, slice(None), lanes(k)).astype(BF16)

            loop(NX, one)

    @pl.when(any_root)
    def _():
        for i in range(2):
            stage[i].wait()
            swap[i].wait_recv()
        loop(ROUNDS, first_blocks)

    def remote(rnd, j, step, way, slot, count=1):
        p = STEPS * j + step
        ref = val.at[pl.ds(rnd * 2 * NS + base + p, count)]
        return pltpu.make_async_remote_copy(
            ref, ref, send_sem.at[rnd, j, slot], recv_sem.at[rnd, p],
            device_id=(nbr[way], t), device_id_type=MESH,
        )

    def to_sib(rnd, j, step, first, count):
        ref = val.at[pl.ds(rnd * 2 * NS + first + STEPS * j + step, count)]
        return pltpu.make_async_remote_copy(
            ref, ref, sib_send.at[rnd], sib_recv.at[rnd, j, step // GROUP],
            device_id=sib, device_id_type=MESH,
        )

    def sends(r, j, rnd, step, count, act):
        a, b, c = r[j], r[(j + 2) % 3], r[(j + 1) % 3]
        level = r[0] + r[1] + r[2]

        @pl.when((level == 0) | (a * (b + c) > 0))
        def _():
            act(remote(rnd, j, step, j, 0, count))

        @pl.when(a * (1 - b) == 1)
        def _():
            act(remote(rnd, j, step, (j + 2) % 3, 1, count))

        @pl.when(a * (1 - b) * (1 - c) == 1)
        def _():
            act(remote(rnd, j, step, (j + 1) % 3, 2, count))

    def exchange(rnd, k, src, dst):
        return pltpu.make_async_remote_copy(
            src, dst, gram_send.at[rnd, k], gram_recv.at[rnd, k],
            device_id=(dp, (t + k + 1) % 8), device_id_type=MESH,
        )

    def all_tiles(rnd, k):
        return exchange(rnd, k, slabs.at[k, rnd], slabs.at[k, rnd])

    def body(tau, carry):
        def forward(rnd):
            r = place(rnd)
            level = r[0] + r[1] + r[2]
            for j in range(3):
                step = tau - OFFS * rnd - SKEW * depth_at(level, r[j])

                @pl.when((step >= 0) & (3 * step + j < NS))
                def _(step=step, j=j):
                    @pl.when(level > 0)
                    def _():
                        remote(rnd, j, step, j, 0).wait_recv()

                    sends(r, j, rnd, step, 1, lambda c: c.start())

                    @pl.when(step % GROUP == GROUP - 1)
                    def _():
                        to_sib(rnd, j, step - (GROUP - 1), base, GROUP).start()

                    @pl.when(step == STEPS - 1)
                    def _():
                        to_sib(rnd, j, STEPS - 1, base, 1).start()

        loop(ROUNDS, forward)

        @pl.when(tau == 0)
        def _():
            for c in loads:
                c.wait()

            def one(i):
                home, k = i // NX, i % NX
                cand[home * NS + slot_of(k)] = rx[:, lanes(i)]
                cand[home * NS + slot_of(NX + k)] = ry[:, lanes(i)]

            loop(2 * NX, one)

            @pl.when(any_root)
            def _():
                for i in range(2, 5):
                    stage[i].wait()
                    swap[i].wait_recv()

        def derive_one(k, carry):
            @pl.when(any_root)
            def _():
                def one(rnd):
                    @pl.when(sum(place(rnd)) == 0)
                    def _():
                        derive_val(rnd, k)

                loop(ROUNDS, one)

            loop(2, lambda home: derive_cand(home, k))
            return carry

        @pl.when(tau < 7)
        def _():
            lax.fori_loop(
                jnp.clip(3 * tau - 5, 0, NG), jnp.clip(3 * tau - 2, 0, NG), derive_one, 0
            )

        def multiply(c):
            rnd, side = c % 2, c // 2
            r = place(rnd)
            level = r[0] + r[1] + r[2]
            now = tau - OFFS * rnd - SLAG * side

            def one(j):
                a = jnp.where(j == 0, r[0], jnp.where(j == 1, r[1], r[2]))
                step = now - SKEW * depth_at(level, a)
                s = 3 * step + j

                @pl.when((step >= 0) & (s < NS))
                def _():
                    first = jnp.where(side == 0, base, obase) + STEPS * j + step

                    @pl.when((side == 1) & (step % GROUP == 0) & (step < STEPS - 1))
                    def _():
                        to_sib(rnd, j, step, obase, GROUP).wait_recv()

                    @pl.when((side == 1) & (step == STEPS - 1))
                    def _():
                        to_sib(rnd, j, STEPS - 1, obase, 1).wait_recv()

                    kind = jnp.where(
                        s < NX, 0, jnp.where(s < 2 * NX, 1, jnp.where(s < 2 * NX + NG, 2, 3))
                    )
                    acc[rnd, kind] += lax.dot_general(
                        cand[first], val[rnd * 2 * NS + first],
                        (((1,), (1,)), ((), ())), preferred_element_type=F32,
                    )

            @pl.when((now >= 0) & (now < STEPS + 4 * SKEW))
            def _():
                loop(3, one)

        loop(4, multiply)

        def send_tiles(rnd):
            turn = tau - OFFS * rnd - 4 * SKEW - SLAG
            tile = -1
            for i, step in enumerate(TILE_STEPS):
                tile = jnp.where(turn == step, i, tile)

            @pl.when(tile >= 0)
            def _():
                gram[rnd, tile] = acc[rnd, tile].astype(BF16)
                loop(7, lambda k: exchange(
                    rnd, k, gram.at[rnd, tile, rows_of((t + k + 1) % 8)], slabs.at[k, rnd, tile]
                ).start())

        @pl.when(tau >= 4 * SKEW + SLAG)
        def _():
            loop(ROUNDS, send_tiles)

        return carry

    lax.fori_loop(0, OFFS + STEPS + 4 * SKEW + SLAG, body, 0)

    token = lax.broadcasted_iota(jnp.int32, (8, ROWS), 1) + t * ROWS
    label = lax.broadcasted_iota(jnp.int32, (8, ROWS), 0)
    row8 = lax.broadcasted_iota(jnp.int32, (8, 128), 0)
    col8 = lax.broadcasted_iota(jnp.int32, (8, 128), 1)
    vtok = lax.broadcasted_iota(jnp.int32, (8, TOK), 1)
    vlab = lax.broadcasted_iota(jnp.int32, (128, TOK), 0)
    cand_hot = jnp.zeros((8, ROWS), F32)
    n_rows = jnp.ones((8, 128), F32)
    start = jnp.int32(0)
    for i in range(8):
        n = cand_len[0, i]
        inside = (label == i) & (token >= start) & (token < start + n)
        cand_hot = jnp.where(inside, 1.0, cand_hot)
        n_rows = jnp.where(row8 == i, n.astype(F32), n_rows)
        start = start + n

    def finish(rnd):
        r = place(rnd)
        for j in range(3):
            sends(r, j, rnd, 0, (NS - j + 2) // 3, lambda c: c.wait_send())
        to_sib(rnd, 0, 0, base, NS).wait_send()

    loop(ROUNDS, finish)

    @pl.when(any_root)
    def _():
        for c in swap:
            c.wait_send()

    def score(rnd):
        segment = jnp.zeros((8, TOK), jnp.int32)
        m_cols = jnp.ones((8, 128), F32)
        bound = jnp.int32(0)
        owner = meta[rnd]
        for i in range(8):
            m = val_len[i, owner]
            bound = bound + m
            segment = segment + jnp.where(vtok >= bound, 1, 0)
            m_cols = jnp.where(col8 == i, m.astype(F32), m_cols)
        hot = jnp.where(vlab == segment[0:1], 1.0, 0.0).astype(F32)
        norm[rnd] = (1.0 / math.sqrt(D * FF)) / jnp.sqrt(n_rows * m_cols)
        loop(7, lambda k: all_tiles(rnd, k).wait_recv())
        total = lax.fori_loop(
            0, 7, lambda k, v: v + slabs[k, rnd].astype(F32), acc[rnd, :, rows_of(t), :]
        )
        pair = total[0] * total[3] + total[2] * total[1]
        cols = lax.dot_general(
            pair, hot, (((1,), (1,)), ((), ())),
            precision=lax.Precision.HIGHEST, preferred_element_type=F32,
        )
        parts[t, rnd] = jnp.dot(
            cand_hot, cols, precision=lax.Precision.HIGHEST, preferred_element_type=F32
        )

    loop(ROUNDS, score)

    def part(k, source):
        return pltpu.make_async_remote_copy(
            parts.at[source], parts.at[source], part_send.at[k], part_recv.at[k],
            device_id=(dp, (t + k + 1) % 8), device_id_type=MESH,
        )

    loop(7, lambda k: part(k, t).start())
    loop(ROUNDS, lambda rnd: loop(7, lambda k: all_tiles(rnd, k).wait_send()))
    loop(7, lambda k: part(k, (t + 7 - k) % 8).wait_recv())
    scores = []
    for rnd in range(ROUNDS):
        total = parts[0, rnd]
        for k in range(1, 8):
            total = total + parts[k, rnd]
        scores.append((total * norm[rnd])[:, :8])
    swapped = jnp.full((8, 8), meta[2], jnp.int32) == 1
    out_ref[0] = jnp.where(swapped, scores[1], scores[0])
    out_ref[1] = jnp.where(swapped, scores[0], scores[1])
    loop(7, lambda k: part(k, t).wait_send())


def spread(number, chips, meta, cand_len, val_len, *arrays):
    any_spec = pl.BlockSpec(memory_space=pl.ANY)
    smem = pl.BlockSpec(memory_space=pltpu.SMEM)
    return pl.pallas_call(
        functools.partial(kernel, chips),
        out_shape=jax.ShapeDtypeStruct((ROUNDS, 8, 8), F32),
        in_specs=[smem] * 3 + [any_spec] * 10,
        out_specs=pl.BlockSpec(memory_space=pltpu.VMEM),
        scratch_shapes=[pltpu.VMEM((TOK, 2 * NG * W), BF16)] * 3
        + [pltpu.VMEM((TOK, 2 * NX * W), BF16)] * 2
        + [pltpu.VMEM((2, TOK, NG * W), BF16)] * 3
        + [pltpu.VMEM((2, TOK, NX * W), BF16)] * 2
        + [
            pltpu.VMEM((2 * NS, TOK, W), BF16),
            pltpu.VMEM((ROUNDS * 2 * NS, TOK, W), BF16),
            pltpu.VMEM((ROUNDS, 4, TOK, TOK), F32),
            pltpu.VMEM((ROUNDS, 4, TOK, TOK), BF16),
            pltpu.VMEM((7, ROUNDS, 4, ROWS, TOK), BF16),
            pltpu.VMEM((8, ROUNDS, 8, 128), F32),
            pltpu.VMEM((ROUNDS, 8, 128), F32),
            pltpu.SemaphoreType.DMA((5,)),
            pltpu.SemaphoreType.DMA((5,)),
            pltpu.SemaphoreType.DMA((5,)),
            pltpu.SemaphoreType.DMA((5,)),
            pltpu.SemaphoreType.DMA((ROUNDS, NS)),
            pltpu.SemaphoreType.DMA((ROUNDS, 3, (STEPS - 1) // GROUP + 1)),
            pltpu.SemaphoreType.DMA((ROUNDS,)),
            pltpu.SemaphoreType.DMA((ROUNDS, 3, 3)),
            pltpu.SemaphoreType.DMA((ROUNDS, 7)),
            pltpu.SemaphoreType.DMA((ROUNDS, 7)),
            pltpu.SemaphoreType.DMA((7,)),
            pltpu.SemaphoreType.DMA((7,)),
        ],
        compiler_params=pltpu.CompilerParams(
            collective_id=number, has_side_effects=True, vmem_limit_bytes=56 * 2**20
        ),
        name="spread",
    )(meta, cand_len, val_len, *arrays)


PAIRS = [(a, b) for a in range(8) for b in range(a, 8)]


def local(*args):
    arrays = args[:10]
    cand_len, val_len, owner = args[10:]
    low, high = jnp.minimum(owner[0], owner[1]), jnp.maximum(owner[0], owner[1])
    meta = jnp.stack([low, high, (owner[0] > owner[1]).astype(jnp.int32)])
    a, b = low >> 1, high >> 1
    index = 8 * a - ((a * (a - 1)) >> 1) + b - a
    branches = [functools.partial(spread, i, chips) for i, chips in enumerate(PAIRS)]
    return lax.switch(index, branches, meta, cand_len, val_len.T, *arrays)


def solution(mesh):
    tile = P("dp", "tensor")
    in_specs = (tile,) * 10 + (P("dp", None), P(), P())
    return jax.shard_map(
        local, mesh=mesh, in_specs=in_specs, out_specs=P(None, "dp", None), check_vma=False
    )
```

```python
import functools
import math

import jax
import jax.numpy as jnp
import numpy as np
from jax import lax
from jax.experimental import pallas as pl
from jax.experimental.pallas import tpu as pltpu
from jax.sharding import PartitionSpec as P

D = 8192
FF = 28672
ROUNDS = 2
TOK = 256
ROWS = TOK // 8
W = 128
NX = 4
NG = 14
NS = 2 * NX + 3 * NG
STEPS = (NS + 2) // 3
SKEW = 3
GROUP = 4
SLAG = GROUP + 1
OFFS = 3
CHUNK = 128
TILE_STEPS = ((NX - 1) // 3, (2 * NX - 1) // 3, (2 * NX + NG - 1) // 3, STEPS - 1)
MESH = pl.DeviceIdType.MESH
F32 = jnp.float32
BF16 = jnp.bfloat16


def derive(gate, up, grad):
    sig = jax.nn.sigmoid(gate)
    act = gate * sig
    hidden = (act * up).astype(BF16)
    grad_gate = (grad * up * sig * (1.0 + gate * (1.0 - sig))).astype(BF16)
    grad_up = (grad * act).astype(BF16)
    return hidden, grad_gate, grad_up


def lanes(block):
    return pl.ds(pl.multiple_of(block * W, W), W)


def rows_of(p):
    return pl.ds(pl.multiple_of(p * ROWS, ROWS), ROWS)


def slot_of(s):
    return STEPS * (s % 3) + s // 3


def loop(count, function):
    def step(i, carry):
        function(i)
        return carry

    lax.fori_loop(0, count, step, 0)


def kernel(
    chips,
    owners, cand_len, val_len,
    cg, cu, cd, cx, cy,
    vg, vu, vd, vx, vy,
    out_ref,
    rg, ru, rd, rx, ry,
    sg, su, sd, sx, sy,
    cand, val, acc, gram, slabs, parts, norm,
    load_sem, stage_sem, swap_send, swap_recv,
    recv_sem, sib_recv, sib_send, send_sem,
    gram_send, gram_recv, part_send, part_recv,
):
    dp = lax.axis_index("dp")
    t = lax.axis_index("tensor")
    core = dp % 2
    x = (dp // 2) % 4
    yh = dp // 8
    bits = ((x // 2 + x % 2) % 2, x // 2, yh)
    nbr = [
        yh * 8 + (x + 1 - 2 * (x % 2)) * 2 + core,
        yh * 8 + (3 - x) * 2 + core,
        (1 - yh) * 8 + x * 2 + core,
    ]
    sib = (yh * 8 + x * 2 + 1 - core, t)
    base = core * NS
    obase = (1 - core) * NS

    places = []
    for chip in chips:
        ox, oy = chip % 4, chip // 4
        obits = ((ox // 2 + ox % 2) % 2, ox // 2, oy)
        places.append([(b + o) % 2 for b, o in zip(bits, obits)])
    any_root = (places[0][0] + places[0][1] + places[0][2]) * (
        places[1][0] + places[1][1] + places[1][2]
    ) == 0

    def place(rnd):
        return [jnp.where(rnd == 0, p, q) for p, q in zip(*places)]

    low = jnp.minimum(owners[0], owners[1])
    high = jnp.maximum(owners[0], owners[1])

    def owner_of(rnd):
        return jnp.where(rnd == 0, low, high)

    def turned(items, j):
        p, q, r = items
        first = jnp.where(j == 0, p, jnp.where(j == 1, q, r))
        second = jnp.where(j == 0, r, jnp.where(j == 1, p, q))
        third = jnp.where(j == 0, q, jnp.where(j == 1, r, p))
        return first, second, third

    def depth_at(level, a):
        return jnp.where(level == 0, 0, level + 2 - 2 * a)

    def half(ref, home, n):
        return ref.at[:, pl.ds(pl.multiple_of(home * (n * W), W), n * W)]

    raw = ((vx, sx, NX), (vy, sy, NX), (vg, sg, NG), (vu, su, NG), (vd, sd, NG))
    stage = [
        pltpu.make_async_copy(half(a, core, n), b.at[0], stage_sem.at[i])
        for i, (a, b, n) in enumerate(raw)
    ]
    swap = [
        pltpu.make_async_remote_copy(
            half(a, 1 - core, n), b.at[1], swap_send.at[i], swap_recv.at[i],
            device_id=sib, device_id_type=MESH,
        )
        for i, (a, b, n) in enumerate(raw)
    ]
    loads = [
        pltpu.make_async_copy(a, b, load_sem.at[i])
        for i, (a, b) in enumerate(((cx, rx), (cy, ry), (cg, rg), (cu, ru), (cd, rd)))
    ]

    @pl.when(any_root)
    def _():
        for c in stage:
            c.start()

    for c in loads:
        c.start()

    def signal(n):
        pl.semaphore_signal(barrier, inc=1, device_id=n, device_id_type=MESH)

    barrier = pltpu.get_barrier_semaphore()
    for n in nbr:
        signal((n, t))
    signal(sib)
    loop(7, lambda k: signal((dp, (t + k + 1) % 8)))

    def clear(i):
        acc[i // 4, i % 4] = jnp.zeros((TOK, TOK), F32)

    loop(8, clear)
    pl.semaphore_wait(barrier, 11)

    @pl.when(any_root)
    def _():
        for c in swap:
            c.start()

    def mine(rnd):
        return jnp.where(owner_of(rnd) % 2 == core, 1.0, 0.0).astype(F32)

    def pick(m, ref, rows, cols):
        own = ref[0, rows, cols].astype(F32)
        other = ref[1, rows, cols].astype(F32)
        return own * m + other * (1.0 - m)

    def put(ref, first, k, rows, blocks):
        h, g, u = blocks
        ref[first + slot_of(2 * NX + k), rows, :] = h
        ref[first + slot_of(2 * NX + NG + 2 * k), rows, :] = g
        ref[first + slot_of(2 * NX + NG + 2 * k + 1), rows, :] = u

    def chunk(i):
        return pl.ds(pl.multiple_of(i * CHUNK, CHUNK), CHUNK)

    def derive_val(rnd, k):
        m = mine(rnd)

        def one(i):
            rows, cols = chunk(i), lanes(k)
            blocks = derive(*(pick(m, ref, rows, cols) for ref in (sg, su, sd)))
            put(val, rnd * 2 * NS + base, k, rows, blocks)

        loop(TOK // CHUNK, one)

    def derive_cand(home, k):
        def one(i):
            rows, cols = chunk(i), lanes(home * NG + k)
            blocks = derive(*(ref[rows, cols].astype(F32) for ref in (rg, ru, rd)))
            put(cand, home * NS, k, rows, blocks)

        loop(TOK // CHUNK, one)

    def first_blocks(rnd):
        m = mine(rnd)

        @pl.when(sum(place(rnd)) == 0)
        def _():
            def one(k):
                first = rnd * 2 * NS + base

                def some(i):
                    rows = chunk(i)
                    val[first + slot_of(k), rows, :] = pick(m, sx, rows, lanes(k)).astype(BF16)
                    val[first + slot_of(NX + k), rows, :] = pick(m, sy, rows, lanes(k)).astype(BF16)

                loop(TOK // CHUNK, some)

            loop(NX, one)

    @pl.when(any_root)
    def _():
        for i in range(2):
            stage[i].wait()
            swap[i].wait_recv()
        loop(ROUNDS, first_blocks)

    def remote(rnd, j, step, way, slot, count=1):
        p = STEPS * j + step
        ref = val.at[pl.ds(rnd * 2 * NS + base + p, count)]
        return pltpu.make_async_remote_copy(
            ref, ref, send_sem.at[rnd, j, slot], recv_sem.at[rnd, p],
            device_id=(way, t), device_id_type=MESH,
        )

    def to_sib(rnd, j, step, first, count):
        ref = val.at[pl.ds(rnd * 2 * NS + first + STEPS * j + step, count)]
        return pltpu.make_async_remote_copy(
            ref, ref, sib_send.at[rnd], sib_recv.at[rnd, j, step // GROUP],
            device_id=sib, device_id_type=MESH,
        )

    def sends(r, j, rnd, step, count, act):
        a, b, c = turned(r, j)
        ways = turned(nbr, j)
        level = a + b + c

        @pl.when((level == 0) | (a * (b + c) > 0))
        def _():
            act(remote(rnd, j, step, ways[0], 0, count))

        @pl.when(a * (1 - b) == 1)
        def _():
            act(remote(rnd, j, step, ways[1], 1, count))

        @pl.when(a * (1 - b) * (1 - c) == 1)
        def _():
            act(remote(rnd, j, step, ways[2], 2, count))

    def exchange(rnd, k, src, dst):
        return pltpu.make_async_remote_copy(
            src, dst, gram_send.at[rnd, k], gram_recv.at[rnd, k],
            device_id=(dp, (t + k + 1) % 8), device_id_type=MESH,
        )

    def all_tiles(rnd, k):
        return exchange(rnd, k, slabs.at[k, rnd], slabs.at[k, rnd])

    def body(tau, carry):
        def forward(rnd, r, level, j):
            step = tau - OFFS * rnd - SKEW * depth_at(level, turned(r, j)[0])

            @pl.when((step >= 0) & (3 * step + j < NS))
            def _():
                @pl.when(level > 0)
                def _():
                    remote(rnd, j, step, sib[0], 0).wait_recv()

                sends(r, j, rnd, step, 1, lambda c: c.start())

                @pl.when(step % GROUP == GROUP - 1)
                def _():
                    to_sib(rnd, j, step - (GROUP - 1), base, GROUP).start()

                @pl.when(step == STEPS - 1)
                def _():
                    to_sib(rnd, j, STEPS - 1, base, 1).start()

        def multiply(rnd, r, level, j, side):
            now = tau - OFFS * rnd - SLAG * side
            step = now - SKEW * depth_at(level, turned(r, j)[0])
            s = 3 * step + j

            @pl.when((step >= 0) & (s < NS))
            def _():
                first = jnp.where(side == 0, base, obase) + STEPS * j + step

                @pl.when((side == 1) & (step % GROUP == 0) & (step < STEPS - 1))
                def _():
                    to_sib(rnd, j, step, obase, GROUP).wait_recv()

                @pl.when((side == 1) & (step == STEPS - 1))
                def _():
                    to_sib(rnd, j, STEPS - 1, obase, 1).wait_recv()

                kind = jnp.where(
                    s < NX, 0, jnp.where(s < 2 * NX, 1, jnp.where(s < 2 * NX + NG, 2, 3))
                )
                acc[rnd, kind] += lax.dot_general(
                    cand[first], val[rnd * 2 * NS + first],
                    (((1,), (1,)), ((), ())), preferred_element_type=F32,
                )

        def turn(rnd):
            r = place(rnd)
            level = r[0] + r[1] + r[2]

            def one(j):
                forward(rnd, r, level, j)

                @pl.when((tau == 0) & (rnd == 0) & (j == 0))
                def _():
                    take_loads()

                loop(2, lambda side: multiply(rnd, r, level, j, side))

            now = tau - OFFS * rnd

            @pl.when((now >= 0) & (now < STEPS + 4 * SKEW + SLAG))
            def _():
                loop(3, one)

        def take_loads():
            for c in loads:
                c.wait()

            def one(i):
                home, k = i // NX, i % NX
                cand[home * NS + slot_of(k)] = rx[:, lanes(i)]
                cand[home * NS + slot_of(NX + k)] = ry[:, lanes(i)]

            loop(2 * NX, one)

            @pl.when(any_root)
            def _():
                for i in range(2, 5):
                    stage[i].wait()
                    swap[i].wait_recv()

        loop(ROUNDS, turn)

        def derive_one(k, carry):
            @pl.when(any_root)
            def _():
                def one(rnd):
                    @pl.when(sum(place(rnd)) == 0)
                    def _():
                        derive_val(rnd, k)

                loop(ROUNDS, one)

            loop(2, lambda home: derive_cand(home, k))
            return carry

        @pl.when(tau < 7)
        def _():
            some = jnp.clip(3 * tau - 5, 0, NG), jnp.clip(3 * tau - 2, 0, NG)
            whole = jnp.where(tau == 0, 0, NG)
            lax.fori_loop(
                jnp.where(any_root, some[0], whole), jnp.where(any_root, some[1], NG), derive_one, 0
            )

        def send_tiles(rnd):
            turn = tau - OFFS * rnd - 4 * SKEW - SLAG
            tile = -1
            for i, step in enumerate(TILE_STEPS):
                tile = jnp.where(turn == step, i, tile)

            @pl.when(tile >= 0)
            def _():
                gram[rnd, tile] = acc[rnd, tile].astype(BF16)
                loop(7, lambda k: exchange(
                    rnd, k, gram.at[rnd, tile, rows_of((t + k + 1) % 8)], slabs.at[k, rnd, tile]
                ).start())

        @pl.when(tau >= 4 * SKEW + SLAG)
        def _():
            loop(ROUNDS, send_tiles)

        return carry

    lax.fori_loop(0, OFFS + STEPS + 4 * SKEW + SLAG, body, 0)

    token = lax.broadcasted_iota(jnp.int32, (8, ROWS), 1) + t * ROWS
    label = lax.broadcasted_iota(jnp.int32, (8, ROWS), 0)
    row8 = lax.broadcasted_iota(jnp.int32, (8, 128), 0)
    col8 = lax.broadcasted_iota(jnp.int32, (8, 128), 1)
    vtok = lax.broadcasted_iota(jnp.int32, (8, TOK), 1)
    vlab = lax.broadcasted_iota(jnp.int32, (128, TOK), 0)
    cand_hot = jnp.zeros((8, ROWS), F32)
    n_rows = jnp.ones((8, 128), F32)
    start = jnp.int32(0)
    for i in range(8):
        n = cand_len[0, i]
        inside = (label == i) & (token >= start) & (token < start + n)
        cand_hot = jnp.where(inside, 1.0, cand_hot)
        n_rows = jnp.where(row8 == i, n.astype(F32), n_rows)
        start = start + n

    def finish(rnd):
        r = place(rnd)
        for j in range(3):
            sends(r, j, rnd, 0, (NS - j + 2) // 3, lambda c: c.wait_send())
        to_sib(rnd, 0, 0, base, NS).wait_send()

    loop(ROUNDS, finish)

    @pl.when(any_root)
    def _():
        for c in swap:
            c.wait_send()

    def score(rnd):
        segment = jnp.zeros((8, TOK), jnp.int32)
        m_cols = jnp.ones((8, 128), F32)
        bound = jnp.int32(0)
        owner = owner_of(rnd)
        for i in range(8):
            m = val_len[i, owner]
            bound = bound + m
            segment = segment + jnp.where(vtok >= bound, 1, 0)
            m_cols = jnp.where(col8 == i, m.astype(F32), m_cols)
        hot = jnp.where(vlab == segment[0:1], 1.0, 0.0).astype(F32)
        norm[rnd] = (1.0 / math.sqrt(D * FF)) / jnp.sqrt(n_rows * m_cols)
        loop(7, lambda k: all_tiles(rnd, k).wait_recv())
        total = lax.fori_loop(
            0, 7, lambda k, v: v + slabs[k, rnd].astype(F32), acc[rnd, :, rows_of(t), :]
        )
        pair = total[0] * total[3] + total[2] * total[1]
        cols = lax.dot_general(
            pair, hot, (((1,), (1,)), ((), ())),
            precision=lax.Precision.HIGHEST, preferred_element_type=F32,
        )
        parts[t, rnd] = jnp.dot(
            cand_hot, cols, precision=lax.Precision.HIGHEST, preferred_element_type=F32
        )

    loop(ROUNDS, score)

    def part(k, source):
        return pltpu.make_async_remote_copy(
            parts.at[source], parts.at[source], part_send.at[k], part_recv.at[k],
            device_id=(dp, (t + k + 1) % 8), device_id_type=MESH,
        )

    loop(7, lambda k: part(k, t).start())
    loop(ROUNDS, lambda rnd: loop(7, lambda k: all_tiles(rnd, k).wait_send()))
    loop(7, lambda k: part(k, (t + 7 - k) % 8).wait_recv())
    scores = []
    for rnd in range(ROUNDS):
        total = parts[0, rnd]
        for k in range(1, 8):
            total = total + parts[k, rnd]
        scores.append((total * norm[rnd])[:, :8])
    swapped = jnp.full((8, 8), owners[0], jnp.int32) > jnp.full((8, 8), owners[1], jnp.int32)
    out_ref[0] = jnp.where(swapped, scores[1], scores[0])
    out_ref[1] = jnp.where(swapped, scores[0], scores[1])
    loop(7, lambda k: part(k, t).wait_send())


def spread(number, chips, owners, cand_len, val_len, *arrays):
    any_spec = pl.BlockSpec(memory_space=pl.ANY)
    smem = pl.BlockSpec(memory_space=pltpu.SMEM)
    return pl.pallas_call(
        functools.partial(kernel, chips),
        out_shape=jax.ShapeDtypeStruct((ROUNDS, 8, 8), F32),
        in_specs=[smem] * 3 + [any_spec] * 10,
        out_specs=pl.BlockSpec(memory_space=pltpu.VMEM),
        scratch_shapes=[pltpu.VMEM((TOK, 2 * NG * W), BF16)] * 3
        + [pltpu.VMEM((TOK, 2 * NX * W), BF16)] * 2
        + [pltpu.VMEM((2, TOK, NG * W), BF16)] * 3
        + [pltpu.VMEM((2, TOK, NX * W), BF16)] * 2
        + [
            pltpu.VMEM((2 * NS, TOK, W), BF16),
            pltpu.VMEM((ROUNDS * 2 * NS, TOK, W), BF16),
            pltpu.VMEM((ROUNDS, 4, TOK, TOK), F32),
            pltpu.VMEM((ROUNDS, 4, TOK, TOK), BF16),
            pltpu.VMEM((7, ROUNDS, 4, ROWS, TOK), BF16),
            pltpu.VMEM((8, ROUNDS, 8, 128), F32),
            pltpu.VMEM((ROUNDS, 8, 128), F32),
            pltpu.SemaphoreType.DMA((5,)),
            pltpu.SemaphoreType.DMA((5,)),
            pltpu.SemaphoreType.DMA((5,)),
            pltpu.SemaphoreType.DMA((5,)),
            pltpu.SemaphoreType.DMA((ROUNDS, NS)),
            pltpu.SemaphoreType.DMA((ROUNDS, 3, (STEPS - 1) // GROUP + 1)),
            pltpu.SemaphoreType.DMA((ROUNDS,)),
            pltpu.SemaphoreType.DMA((ROUNDS, 3, 3)),
            pltpu.SemaphoreType.DMA((ROUNDS, 7)),
            pltpu.SemaphoreType.DMA((ROUNDS, 7)),
            pltpu.SemaphoreType.DMA((7,)),
            pltpu.SemaphoreType.DMA((7,)),
        ],
        compiler_params=pltpu.CompilerParams(
            collective_id=number, has_side_effects=True, vmem_limit_bytes=56 * 2**20
        ),
        name="spread",
    )(owners, cand_len, val_len, *arrays)


PAIRS = [(a, b) for a in range(8) for b in range(a, 8)]
BRANCH = np.array(
    [PAIRS.index(tuple(sorted((p // 2, q // 2)))) for p in range(16) for q in range(16)], np.int32
)


def local(*args):
    arrays = args[:10]
    cand_len, val_len, owner = args[10:]
    index = jnp.asarray(BRANCH)[owner[0] * 16 + owner[1]]
    branches = [functools.partial(spread, i, chips) for i, chips in enumerate(PAIRS)]
    return lax.switch(index, branches, owner, cand_len, val_len.T, *arrays)


def solution(mesh):
    tile = P("dp", "tensor")
    in_specs = (tile,) * 10 + (P("dp", None), P(), P())
    return jax.shard_map(
        local, mesh=mesh, in_specs=in_specs, out_specs=P(None, "dp", None), check_vma=False
    )
```
